32 devices in a mesh: section: 2 (over x), dp: 4 (over z), ctx: 4 (over y, core).
Axes of the slice: x: 2, y: 2, z: 4, core: 2. Of those that a mesh axis runs over, the one named last changes fastest.
Arguments:
- tokens: bfloat16 [8, 1024, 768], P('dp', 'ctx'), may hold values from -6 to 6
- qkv_weight: float32 [2, 768, 2304], P('section', ('dp', 'ctx')), may hold values from -0.21875 to 0.21875
- out_weight: float32 [2, 768, 768], P('section', ('dp', 'ctx')), may hold values from -1.75 to 1.75
- up_weight: float32 [2, 768, 3072], P('section', ('dp', 'ctx')), may hold values from -0.21875 to 0.21875
- down_weight: float32 [2, 3072, 768], P('section', ('dp', 'ctx')), may hold values from -0.109375 to 0.109375
- norm_gain: float32 [2, 2, 768], P('section', None, ('dp', 'ctx')), may hold values from 0.1 to 1.9
- norm_bias: float32 [2, 2, 768], P('section', None, ('dp', 'ctx')), may hold values from -3 to 3
- random_blocks: int32 [2, 8, 16, 12, 3], P('section', 'dp'), may hold values from 0 to 15, as said below
- targets: bfloat16 [8, 1024, 768], P('dp', 'ctx'), may hold values from -5 to 5
- mask_pos: int32 [8, 512], P('dp'), may hold values from 0 to 1023, as said below
- mask_count: int32 [8], P('dp'), may hold values from 256 to 512
Outputs:
- layer_outputs: float32 [2, 8, 1024, 768], P('section', 'dp', 'ctx')
- input_grads: float32 [2, 8, 1024, 768], P('section', 'dp', 'ctx')
- qkv_grad: float32 [2, 768, 2304], P('section', ('dp', 'ctx'))
- out_grad: float32 [2, 768, 768], P('section', ('dp', 'ctx'))
- up_grad: float32 [2, 768, 3072], P('section', ('dp', 'ctx'))
- down_grad: float32 [2, 3072, 768], P('section', ('dp', 'ctx'))
- gain_grad: float32 [2, 2, 768], P('section', None, ('dp', 'ctx'))
- bias_grad: float32 [2, 2, 768], P('section', None, ('dp', 'ctx'))
The draws below stay inside these ranges and needn't reach their ends.
Inputs may be any that keep to these rules, and one draw needn't show every extreme that they name: `random_blocks`: for each layer and sequence, the 144 entries of the 4 consecutive query blocks held by one index of ctx (all heads and draws) name the 4 blocks held by any one index of ctx at least 35 and at most 36 times. `mask_pos`: the 512 positions of a sequence are distinct; the first mask_count of them are the masked ones.
All inputs are finite; a program needn't handle non-finite values.
Results may differ from the reference program's by a relative error of at most 0.018.
The reference program's roundings to bfloat16 on the way count: a program that leaves them out, or rounds other values in their place, can miss the bound.
Values may be sent and summed in bfloat16 or wider, within the bound.
No kernel may reach another device: no remote copies, remote signals or barrier semaphores. Data moves between devices by JAX's collectives and lax.ppermute only.
A program may use at most 256 MiB of HBM per device.

```python
import math
import jax
import jax.numpy as jnp
from jax import lax

D = 768
HEADS = 12
HEAD_DIM = 64
FF = 3072
BLOCK = 64
RAND = 3
LAYERS = 2
SEQ = 1024
SEQS = 8
NB = 16
NBD = 4
SLOTS = 144
MAXM = 512
N_CTX = 4


def draw_random_blocks(key, part):
    key_one, key_two, key_three = jax.random.split(key, 3)
    scores = jax.random.randint(key_one, (LAYERS, SEQS, N_CTX, SLOTS), 0, 1 << 20) * SLOTS + jnp.arange(SLOTS, dtype=jnp.int32)
    ordering = jnp.argsort(scores, axis=-1, stable=True).astype(jnp.int32)
    offset = jax.random.randint(key_two, (LAYERS, SEQS, N_CTX, 1), 0, N_CTX)
    holder = (ordering + offset) % N_CTX
    inside = jax.random.randint(key_three, (LAYERS, SEQS, N_CTX, SLOTS), 0, NBD)
    blocks = holder * NBD + inside
    return blocks.reshape(LAYERS, SEQS, NB, HEADS, RAND).astype(jnp.int32)


def draw_mask_pos(key, part):
    scores = jax.random.randint(key, (SEQS, SEQ), 0, 1 << 14) * SEQ + jnp.arange(SEQ, dtype=jnp.int32)
    ordering = jnp.argsort(scores, axis=-1, stable=True).astype(jnp.int32)
    return ordering[:, :MAXM]


def with_ends(values, key, low, largest):
    longest = values.shape.index(max(values.shape))
    spots = []
    for shift in (0, 1):
        where = [jax.random.randint(jax.random.fold_in(key, axis), (), 0, length) for axis, length in enumerate(values.shape)]
        where[longest] = (where[longest] + shift) % values.shape[longest]
        spots.append(tuple(where))
    return values.at[spots[0]].set(low).at[spots[1]].set(largest)


def block_scale(rng, dims, pieces, low, top_value):
    factor_of = 1.0
    for dim, shards_of in pieces:
        steps = jax.random.uniform(jax.random.fold_in(jax.random.fold_in(rng, 6), dim), (shards_of,), jnp.float32, low / len(pieces), top_value / len(pieces))
        factor_of = factor_of * jnp.repeat(jnp.exp(steps), dims[dim] // shards_of).reshape((-1,) + (1,) * (len(dims) - 1 - dim))
    return factor_of


def centred(key, dims, deviation, reach, shards=(), kind=jnp.bfloat16):
    level = block_scale(key, dims, shards, -0.22, 0.18) if shards else 1.0
    values = jax.random.normal(key, dims, jnp.float32) * deviation * level
    return jnp.minimum(jnp.maximum(values, -reach), reach).astype(kind)


def setup_inputs(seed: int = 0) -> dict:
    splits = jax.random.split(jax.random.key(seed), 12)
    return {
        "tokens": centred(splits[0], (SEQS, SEQ, D), 1.0, 6.0, ((0, 4), (1, 4))),
        "qkv_weight": centred(splits[1], (LAYERS, D, 3 * D), D ** -0.5, 0.21875, ((0, 2), (1, 16)), jnp.float32),
        "out_weight": centred(splits[2], (LAYERS, D, D), (D // 64) ** -0.5, 1.75, ((0, 2), (1, 16)), jnp.float32),
        "up_weight": centred(splits[3], (LAYERS, D, FF), D ** -0.5, 0.21875, ((0, 2), (1, 16)), jnp.float32),
        "down_weight": centred(splits[4], (LAYERS, FF, D), FF ** -0.5, 0.109375, ((0, 2), (1, 16)), jnp.float32),
        "norm_gain": jnp.clip(1.0 + 0.18 * jax.random.normal(splits[5], (LAYERS, 2, D), jnp.float32), 0.1, 1.9),
        "norm_bias": centred(splits[6], (LAYERS, 2, D), 0.5, 3.0, ((0, 2), (2, 16)), jnp.float32),
        "random_blocks": draw_random_blocks(jax.random.fold_in(splits[11], 71), 0),
        "targets": centred(splits[8], (SEQS, SEQ, D), 1.0, 5.0, ((0, 4), (1, 4))),
        "mask_pos": draw_mask_pos(jax.random.fold_in(splits[11], 71), 0),
        "mask_count": with_ends(jax.random.randint(splits[10], (SEQS,), MAXM // 2, MAXM + 1), jax.random.fold_in(splits[10], 1), MAXM // 2, MAXM).astype(jnp.int32),
    }


@jax.custom_vjp
def low(v):
    return lax.optimization_barrier(v.astype(jnp.bfloat16)).astype(jnp.float32)

@jax.custom_vjp
def low_back(v):
    return v

def low_keep(v):
    return (low(v), None)

def low_pass(kept, grad):
    return (grad,)

def back_keep(v):
    return (v, None)

def back_low(kept, grad):
    return (low(grad),)
low.defvjp(low_keep, low_pass)
low_back.defvjp(back_keep, back_low)
norm_epsilon = 1e-06
highest = lax.Precision.HIGHEST

def layer_norm(summed, gain_row, bias_row):
    center = summed - lax.optimization_barrier(jnp.mean(summed, axis=-1, keepdims=True))
    variance = lax.optimization_barrier(jnp.mean(center * center, axis=-1, keepdims=True))
    return center * lax.rsqrt(variance + norm_epsilon) * gain_row + bias_row

def by_blocks(field):
    return field.reshape(field.shape[0] // BLOCK, BLOCK, HEADS, HEAD_DIM).transpose(0, 2, 1, 3)

def block_attention(queries, keys, values, drawn_blocks):
    block_count = queries.shape[0] // BLOCK
    score_scale = 1.0 / math.sqrt(HEAD_DIM)
    query_blocks = by_blocks(queries)
    key_blocks = by_blocks(keys)
    value_blocks = by_blocks(values)
    numbers = jnp.arange(block_count, dtype=jnp.int32)
    window = jnp.clip(numbers[:, None] + jnp.arange(-1, 2, dtype=jnp.int32)[None, :], 0, block_count - 1)
    head_ids = jnp.arange(HEADS, dtype=jnp.int32)
    edge_ids = jnp.array([0, block_count - 1], dtype=jnp.int32)

    def collect(table_in):
        nearby = table_in[window[:, None, :], head_ids[None, :, None]]
        chosen = table_in[drawn_blocks, head_ids[None, :, None]]
        edge_part = jnp.broadcast_to(table_in[edge_ids].transpose(1, 0, 2, 3)[None], (block_count, HEADS, 2, BLOCK, HEAD_DIM))
        joined = jnp.concatenate([nearby, chosen, edge_part], axis=2)
        return joined.reshape(block_count, HEADS, (5 + RAND) * BLOCK, HEAD_DIM)
    listed_keys = collect(key_blocks)
    listed_values = collect(value_blocks)
    scores = low_back(jnp.einsum('nhqe,nhke->nhqk', query_blocks, listed_keys, precision=highest) * score_scale)
    weights = low(jax.nn.softmax(scores, axis=-1))
    sparse = jnp.einsum('nhqk,nhke->nhqe', weights, listed_values, precision=highest)
    edge_queries = query_blocks[edge_ids].transpose(1, 0, 2, 3).reshape(HEADS, 2 * BLOCK, HEAD_DIM)
    all_keys = key_blocks.transpose(1, 0, 2, 3).reshape(HEADS, block_count * BLOCK, HEAD_DIM)
    all_values = value_blocks.transpose(1, 0, 2, 3).reshape(HEADS, block_count * BLOCK, HEAD_DIM)
    wide_scores = low_back(jnp.einsum('hqe,hke->hqk', edge_queries, all_keys, precision=highest) * score_scale)
    wide_weights = low(jax.nn.softmax(wide_scores, axis=-1))
    wide_out = jnp.einsum('hqk,hke->hqe', wide_weights, all_values, precision=highest)
    wide_out = wide_out.reshape(HEADS, 2, BLOCK, HEAD_DIM).transpose(1, 0, 2, 3)
    merged = jnp.concatenate([wide_out[:1], sparse[1:block_count - 1], wide_out[1:]], axis=0)
    return merged.transpose(0, 2, 1, 3).reshape(block_count * BLOCK, HEADS * HEAD_DIM)

def one_layer(inputs, params, drawn_blocks):
    qkv_matrix, out_matrix, up_matrix, down_matrix, gains, biases = params
    projected = low_back(low(jnp.dot(inputs, qkv_matrix, precision=highest)))
    context = block_attention(projected[:, :D], projected[:, D:2 * D], projected[:, 2 * D:], drawn_blocks)
    context = low_back(low(context))
    mixed = low_back(jnp.dot(context, out_matrix, precision=highest))
    middle = layer_norm(inputs + mixed, gains[0], biases[0])
    hidden = low_back(jnp.dot(low(middle), up_matrix, precision=highest))
    active = low(jax.nn.gelu(hidden, approximate=True))
    branch = low_back(jnp.dot(active, down_matrix, precision=highest))
    return layer_norm(middle + branch, gains[1], biases[1])

def reference(tokens, qkv_weight, out_weight, up_weight, down_weight, norm_gain, norm_bias, random_blocks, targets, mask_pos, mask_count):
    masters = (qkv_weight, out_weight, up_weight, down_weight, norm_gain, norm_bias)
    positions = jnp.arange(SEQ, dtype=jnp.int32)
    entries = jnp.arange(MAXM, dtype=jnp.int32)

    def network(params, first_in, padding, drawn_blocks, target, chosen):
        rounded = jax.tree.map(low, params)
        output_one = one_layer(first_in, tuple((member[0] for member in rounded)), drawn_blocks[0])
        second_in = low_back(low(output_one) + padding)
        output_two = one_layer(second_in, tuple((member[1] for member in rounded)), drawn_blocks[1])
        missing = output_two - target
        return (0.5 * jnp.sum(chosen[:, None] * missing * missing), (output_one, output_two))

    def per_sequence(running, sequence):
        first_in, drawn_blocks, target, picked_pos, used_count = sequence
        matches = (picked_pos[None, :] == positions[:, None]) & (entries < used_count)[None, :]
        chosen = lax.optimization_barrier(jnp.sum(matches.astype(jnp.float32), axis=1))
        padding = jnp.zeros((SEQ, D), jnp.float32)
        loss_value, pullback, outputs = jax.vjp(lambda params, start, extra: network(params, start, extra, drawn_blocks, target, chosen), masters, first_in, padding, has_aux=True)
        gradients, grad_first, grad_second = pullback(jnp.ones_like(loss_value))
        running = jax.tree.map(lambda before, gradient: before + gradient, running, gradients)
        return (running, (outputs[0], outputs[1], grad_first, grad_second))
    sequences = (tokens.astype(jnp.float32), jnp.moveaxis(random_blocks, 1, 0), targets.astype(jnp.float32), mask_pos, mask_count)
    zeros_init = jax.tree.map(jnp.zeros_like, masters)
    totals, (output_one, output_two, grad_first, grad_second) = lax.scan(per_sequence, zeros_init, sequences)
    return (jnp.stack([output_one, output_two]), jnp.stack([grad_first, grad_second]), totals[0], totals[1], totals[2], totals[3], totals[4], totals[5])
```

```python
import math

import jax
import jax.numpy as jnp
from jax import lax
from jax.experimental import pallas as pl
from jax.experimental.pallas import tpu as pltpu
from jax.sharding import PartitionSpec as P

D = 768
HEADS = 12
HEAD_DIM = 64
BLOCK = 64
RAND = 3
LISTED = 5 + RAND
PAIR = 2 * HEAD_DIM
PAIRS = HEADS // 2
SHARED = 5 * BLOCK
DRAWN = RAND * BLOCK
SCALE = 1.0 / math.sqrt(HEAD_DIM)

norm_epsilon = 1e-06

NT = (((1,), (1,)), ((), ()))
TN = (((0,), (0,)), ((), ()))


def swap(value, axis, bit):
    count = lax.axis_size(axis)
    return lax.ppermute(value, axis, [(i, i ^ bit) for i in range(count)])


def bits_of(count):
    return [1 << k for k in range(count.bit_length() - 1)]


def spread(piece, axis):
    count = lax.axis_size(axis)
    slots = {0: piece}
    for bit in reversed(bits_of(count)):
        for j in sorted(slots):
            slots[j ^ bit] = swap(slots[j], axis, bit)
    return [slots[j] for j in range(count)]


def gather_rows(shard):
    rows, width = shard.shape
    depth = lax.axis_size("dp")
    count = lax.axis_size("ctx")
    dp_index = lax.axis_index("dp")
    ctx_index = lax.axis_index("ctx")
    column = jnp.zeros((depth, rows, width), shard.dtype)
    for k in range(depth):
        part = shard if k == 0 else swap(shard, "dp", k)
        column = lax.dynamic_update_index_in_dim(column, part, dp_index ^ k, 0)
    whole = jnp.zeros((depth, count, rows, width), shard.dtype)
    for j, part in enumerate(spread(column, "ctx")):
        whole = lax.dynamic_update_index_in_dim(whole, part[:, None], ctx_index ^ j, 1)
    return whole.reshape(depth * count * rows, width)


def scatter_rows(grad):
    depth = lax.axis_size("dp")
    count = lax.axis_size("ctx")
    dp_index = lax.axis_index("dp")
    ctx_index = lax.axis_index("ctx")
    width = grad.shape[1]
    rows = grad.shape[0] // (depth * count)
    field = grad.reshape(depth, count, rows, width)
    slots = {
        j: lax.dynamic_index_in_dim(field, ctx_index ^ j, 1, keepdims=False) for j in range(count)
    }
    for bit in bits_of(count):
        for j in [j for j in slots if j & bit]:
            got = swap(slots.pop(j).astype(jnp.bfloat16), "ctx", bit)
            slots[j ^ bit] = slots[j ^ bit] + got.astype(jnp.float32)
    column = slots[0]
    total = lax.dynamic_index_in_dim(column, dp_index, 0, keepdims=False)
    for k in range(1, depth):
        part = lax.dynamic_index_in_dim(column, dp_index ^ k, 0, keepdims=False)
        total = total + swap(part.astype(jnp.bfloat16), "dp", k).astype(jnp.float32)
    return total


def block_at(ref, index):
    return ref[pl.ds(pl.multiple_of(index * BLOCK, BLOCK), BLOCK), :]


def attend_kernel(ids_ref, global_ref, q_ref, k_ref, v_ref, c_ref):
    pair = pl.program_id(0)
    blocks = q_ref.shape[0] // BLOCK
    low = lax.broadcasted_iota(jnp.int32, (BLOCK, PAIR), 1) < HEAD_DIM

    def step(block, carry):
        rows = pl.ds(pl.multiple_of(block * BLOCK, BLOCK), BLOCK)
        q = q_ref[rows, :]
        blank = jnp.zeros_like(q)
        halves = (jnp.where(low, q, blank), jnp.where(low, blank, q))

        def one(query, keys, values):
            scores = lax.dot_general(query, keys, NT, preferred_element_type=jnp.float32) * SCALE
            peak = jnp.max(scores, axis=-1, keepdims=True)
            raised = jnp.exp(scores - peak)
            total = jnp.sum(raised, axis=-1, keepdims=True)
            weights = (raised * (1.0 / total)).astype(jnp.bfloat16)
            return jnp.dot(weights, values, preferred_element_type=jnp.float32)

        is_global = global_ref[block] == 1

        @pl.when(is_global)
        def _():
            keys = k_ref[...]
            values = v_ref[...]
            first = one(halves[0], keys, values)
            second = one(halves[1], keys, values)
            c_ref[rows, :] = jnp.where(low, first, second).astype(c_ref.dtype)

        @pl.when(jnp.logical_not(is_global))
        def _():
            parts = []
            for half in range(2):
                base = (block * HEADS + 2 * pair + half) * LISTED
                names = [ids_ref[base + j] for j in range(LISTED)]
                keys = jnp.concatenate([block_at(k_ref, n) for n in names], axis=0)
                values = jnp.concatenate([block_at(v_ref, n) for n in names], axis=0)
                parts.append(one(halves[half], keys, values))
            c_ref[rows, :] = jnp.where(low, parts[0], parts[1]).astype(c_ref.dtype)

        return carry

    lax.fori_loop(0, blocks, step, 0)


def attend(ids, is_global, projected, gathered):
    tokens_dev = projected.shape[0]
    everything = gathered.shape[0]
    return pl.pallas_call(
        attend_kernel,
        grid_spec=pltpu.PrefetchScalarGridSpec(
            num_scalar_prefetch=2,
            grid=(PAIRS,),
            in_specs=[
                pl.BlockSpec((tokens_dev, PAIR), lambda p, i, g: (0, p)),
                pl.BlockSpec((everything, PAIR), lambda p, i, g: (0, p)),
                pl.BlockSpec((everything, PAIR), lambda p, i, g: (0, PAIRS + p)),
            ],
            out_specs=pl.BlockSpec((tokens_dev, PAIR), lambda p, i, g: (0, p)),
        ),
        out_shape=jax.ShapeDtypeStruct((tokens_dev, D), jnp.bfloat16),
        name="attend",
    )(ids, is_global, projected, gathered, gathered)


def attend_back_kernel(
    ids_ref,
    global_ref,
    q_ref,
    dc_ref,
    k_ref,
    v_ref,
    dq_ref,
    dk_own_ref,
    dv_own_ref,
    dk_far_ref,
    dv_far_ref,
    dk_ref,
    dv_ref,
):
    pair = pl.program_id(0)
    tokens_dev = q_ref.shape[0]
    blocks = tokens_dev // BLOCK
    low = lax.broadcasted_iota(jnp.int32, (BLOCK, PAIR), 1) < HEAD_DIM
    low_drawn = lax.broadcasted_iota(jnp.int32, (DRAWN, PAIR), 1) < HEAD_DIM
    dk_ref[...] = jnp.zeros_like(dk_ref)
    dv_ref[...] = jnp.zeros_like(dv_ref)

    def step(block, carry):
        rows = pl.ds(pl.multiple_of(block * BLOCK, BLOCK), BLOCK)

        def both(ref):
            part = ref[rows, :]
            blank = jnp.zeros_like(part)
            return jnp.concatenate([jnp.where(low, part, blank), jnp.where(low, blank, part)], axis=0)

        queries = both(q_ref)
        grads = both(dc_ref)

        def weigh(scores, grad_weights):
            peak = jnp.max(scores, axis=0, keepdims=True)
            raised = jnp.exp(scores - peak)
            total = jnp.sum(raised, axis=0, keepdims=True)
            weights = raised * (1.0 / total)
            row_dot = jnp.sum(weights * grad_weights, axis=0, keepdims=True)
            grad_scores = weights * (grad_weights - row_dot)
            return weights.astype(jnp.bfloat16), grad_scores.astype(jnp.bfloat16)

        def times(left, right, dims):
            return lax.dot_general(left, right, dims, preferred_element_type=jnp.float32)

        def keep_query(grad_scores, keys):
            wide = times(grad_scores, keys, TN) * SCALE
            dq_ref[rows, :] = jnp.where(low, wide[:BLOCK], wide[BLOCK:]).astype(dq_ref.dtype)

        is_global = global_ref[block] == 1

        @pl.when(is_global)
        def _():
            keys = k_ref[...]
            weights, grad_scores = weigh(
                times(keys, queries, NT) * SCALE, times(v_ref[...], grads, NT)
            )
            keep_query(grad_scores, keys)
            dk_ref[...] += jnp.dot(grad_scores, queries, preferred_element_type=jnp.float32) * SCALE
            dv_ref[...] += jnp.dot(weights, grads, preferred_element_type=jnp.float32)

        @pl.when(jnp.logical_not(is_global))
        def _():
            base = (block * HEADS + 2 * pair) * LISTED
            names = [ids_ref[base + j] for j in range(LISTED)]
            names += [ids_ref[base + LISTED + j] for j in range(5, LISTED)]
            keys = jnp.concatenate([block_at(k_ref, n) for n in names], axis=0)
            values = jnp.concatenate([block_at(v_ref, n) for n in names], axis=0)

            def merge(full):
                return jnp.concatenate(
                    [
                        full[:SHARED],
                        jnp.where(
                            low_drawn, full[SHARED : SHARED + DRAWN], full[SHARED + DRAWN :]
                        ),
                    ],
                    axis=0,
                )

            def unmerge(full):
                tail = full[SHARED:]
                blank = jnp.zeros_like(tail)
                return jnp.concatenate(
                    [full[:SHARED], jnp.where(low_drawn, tail, blank), jnp.where(low_drawn, blank, tail)],
                    axis=0,
                )

            weights, grad_scores = weigh(
                merge(times(keys, queries, NT)) * SCALE, merge(times(values, grads, NT))
            )
            weights = unmerge(weights)
            grad_scores = unmerge(grad_scores)
            keep_query(grad_scores, keys)
            grad_keys = jnp.dot(grad_scores, queries, preferred_element_type=jnp.float32) * SCALE
            grad_values = jnp.dot(weights, grads, preferred_element_type=jnp.float32)
            for place, name in enumerate(names):
                target = pl.ds(pl.multiple_of(name * BLOCK, BLOCK), BLOCK)
                here = slice(place * BLOCK, (place + 1) * BLOCK)
                dk_ref[target, :] += grad_keys[here]
                dv_ref[target, :] += grad_values[here]

        return carry

    lax.fori_loop(0, blocks, step, 0)
    dk_own_ref[...] = dk_ref[:tokens_dev, :]
    dv_own_ref[...] = dv_ref[:tokens_dev, :]
    dk_far_ref[...] = dk_ref[tokens_dev:, :].astype(dk_far_ref.dtype)
    dv_far_ref[...] = dv_ref[tokens_dev:, :].astype(dv_far_ref.dtype)


def attend_back(ids, is_global, projected, grad_context, gathered):
    tokens_dev = projected.shape[0]
    everything = gathered.shape[0]
    far = everything - tokens_dev

    def at(rows):
        return pl.BlockSpec((rows, PAIR), lambda p, i, g: (0, p))

    return pl.pallas_call(
        attend_back_kernel,
        grid_spec=pltpu.PrefetchScalarGridSpec(
            num_scalar_prefetch=2,
            grid=(PAIRS,),
            in_specs=[
                at(tokens_dev),
                at(tokens_dev),
                at(everything),
                pl.BlockSpec((everything, PAIR), lambda p, i, g: (0, PAIRS + p)),
            ],
            out_specs=[at(tokens_dev), at(tokens_dev), at(tokens_dev), at(far), at(far)],
            scratch_shapes=[
                pltpu.VMEM((everything, PAIR), jnp.float32),
                pltpu.VMEM((everything, PAIR), jnp.float32),
            ],
        ),
        out_shape=[
            jax.ShapeDtypeStruct((tokens_dev, D), jnp.bfloat16),
            jax.ShapeDtypeStruct((tokens_dev, D), jnp.float32),
            jax.ShapeDtypeStruct((tokens_dev, D), jnp.float32),
            jax.ShapeDtypeStruct((far, D), jnp.bfloat16),
            jax.ShapeDtypeStruct((far, D), jnp.bfloat16),
        ],
        name="attend_back",
    )(ids, is_global, projected, grad_context, gathered, gathered)


def return_pairs(own, far):
    tokens_dev = own.shape[0]
    count = lax.axis_size("ctx")
    slots = {0: own}
    for j in range(1, count):
        slots[j] = far[(j - 1) * tokens_dev : j * tokens_dev]
    for bit in bits_of(count):
        for j in [j for j in slots if j & bit]:
            got = swap(slots.pop(j).astype(jnp.bfloat16), "ctx", bit)
            slots[j ^ bit] = slots[j ^ bit].astype(jnp.float32) + got.astype(jnp.float32)
    return slots[0]


def listed_blocks(drawn, ctx_index, group_size):
    block_count = drawn.shape[0]
    per_device = block_count // group_size
    own = ctx_index * per_device + jnp.arange(per_device, dtype=jnp.int32)
    mine = lax.dynamic_slice_in_dim(drawn, ctx_index * per_device, per_device, axis=0)
    near = jnp.clip(
        own[:, None] + jnp.arange(-1, 2, dtype=jnp.int32)[None, :], 0, block_count - 1
    )
    ends = jnp.broadcast_to(jnp.array([0, block_count - 1], jnp.int32)[None], (per_device, 2))
    shared = jnp.concatenate([near, ends], axis=1)
    names = jnp.concatenate(
        [jnp.broadcast_to(shared[:, None], (per_device, HEADS, 5)), mine], axis=2
    )
    places = ((names // per_device) ^ ctx_index) * per_device + names % per_device
    is_global = ((own == 0) | (own == block_count - 1)).astype(jnp.int32)
    return places.reshape(-1), is_global


def normalize(summed):
    center = summed - jnp.mean(summed, axis=-1, keepdims=True)
    inverse = lax.rsqrt(jnp.mean(center * center, axis=-1, keepdims=True) + norm_epsilon)
    return center * inverse, inverse


def normalize_back(scaled_grad, normal, inverse):
    return (
        scaled_grad
        - jnp.mean(scaled_grad, axis=-1, keepdims=True)
        - normal * jnp.mean(scaled_grad * normal, axis=-1, keepdims=True)
    ) * inverse


def gelu_tanh(values):
    return jax.nn.gelu(values, approximate=True)


def dot32(left, right):
    return jnp.dot(left, right, preferred_element_type=jnp.float32)


def dot_nt(left, right):
    return lax.dot_general(left, right, NT, preferred_element_type=jnp.float32)


def dot_tn(left, right):
    return lax.dot_general(left, right, TN, preferred_element_type=jnp.float32)


def layer_forward(inputs, table, weights):
    qkv_matrix, out_matrix, up_matrix, down_matrix, gains, biases = weights
    projected = dot32(inputs, qkv_matrix).astype(jnp.bfloat16)
    gathered = jnp.concatenate(spread(projected[:, D:], "ctx"), axis=0)
    context = attend(*table, projected, gathered)
    first_sum = inputs.astype(jnp.float32) + dot32(context, out_matrix)
    first_normal, first_inverse = normalize(first_sum)
    middle = first_normal * gains[0] + biases[0]
    middle_low = middle.astype(jnp.bfloat16)
    hidden = dot32(middle_low, up_matrix)
    active = gelu_tanh(hidden).astype(jnp.bfloat16)
    second_normal, second_inverse = normalize(middle + dot32(active, down_matrix))
    result = second_normal * gains[1] + biases[1]
    saved = (
        inputs,
        projected,
        gathered,
        context,
        first_normal,
        first_inverse,
        middle_low,
        hidden,
        active,
        second_normal,
        second_inverse,
    )
    return result, saved


def layer_backward(grad_out, saved, table, weights):
    (
        inputs,
        projected,
        gathered,
        context,
        first_normal,
        first_inverse,
        middle_low,
        hidden,
        active,
        second_normal,
        second_inverse,
    ) = saved
    qkv_matrix, out_matrix, up_matrix, down_matrix, gains, biases = weights
    gain_two = jnp.sum(grad_out * second_normal, axis=0)
    bias_two = jnp.sum(grad_out, axis=0)
    grad_second = normalize_back(grad_out * gains[1], second_normal, second_inverse)
    grad_branch = grad_second.astype(jnp.bfloat16)
    down_grad = dot_tn(active, grad_branch)
    grad_active = dot_nt(grad_branch, down_matrix)
    gelu_back = jax.vjp(gelu_tanh, hidden)[1]
    grad_hidden = gelu_back(grad_active)[0].astype(jnp.bfloat16)
    up_grad = dot_tn(middle_low, grad_hidden)
    grad_middle = grad_second + dot_nt(grad_hidden, up_matrix)
    gain_one = jnp.sum(grad_middle * first_normal, axis=0)
    bias_one = jnp.sum(grad_middle, axis=0)
    grad_first = normalize_back(grad_middle * gains[0], first_normal, first_inverse)
    grad_mixed = grad_first.astype(jnp.bfloat16)
    out_grad = dot_tn(context, grad_mixed)
    grad_context = dot_nt(grad_mixed, out_matrix).astype(jnp.bfloat16)
    dq, dk_own, dv_own, dk_far, dv_far = attend_back(
        *table, projected, grad_context, gathered
    )
    dk = return_pairs(dk_own, dk_far).astype(jnp.bfloat16)
    dv = return_pairs(dv_own, dv_far).astype(jnp.bfloat16)
    grad_projected = jnp.concatenate([dq, dk, dv], axis=1)
    qkv_grad = dot_tn(inputs, grad_projected)
    grad_inputs = grad_first + dot_nt(grad_projected, qkv_matrix)
    vectors = jnp.stack([gain_one, gain_two, bias_one, bias_two])
    return grad_inputs, (qkv_grad, out_grad, up_grad, down_grad), vectors


def chosen_rows(picked_pos, used_count, ctx_index, tokens_dev):
    positions = ctx_index * tokens_dev + jnp.arange(tokens_dev, dtype=jnp.int32)
    entries = jnp.arange(picked_pos.shape[0], dtype=jnp.int32)
    matches = (picked_pos[None, :] == positions[:, None]) & (entries < used_count)[None, :]
    return jnp.sum(matches.astype(jnp.float32), axis=1)


def body(
    tokens,
    qkv_weight,
    out_weight,
    up_weight,
    down_weight,
    norm_gain,
    norm_bias,
    random_blocks,
    targets,
    mask_pos,
    mask_count,
):
    section = lax.axis_index("section")
    ctx_index = lax.axis_index("ctx")
    group_size = lax.axis_size("ctx")
    tokens_dev = tokens.shape[1]
    first = section == 0

    def by_layer(own):
        other = swap(own, "section", 1)
        return jnp.where(first, own, other), jnp.where(first, other, own)

    def pick(field):
        return lax.dynamic_index_in_dim(field, section, 0, keepdims=False)

    shards = [
        by_layer(member[0].astype(jnp.bfloat16))
        for member in (qkv_weight, out_weight, up_weight, down_weight)
    ]
    vector_shard = jnp.concatenate([norm_gain[0], norm_bias[0]], axis=0).astype(jnp.bfloat16)
    vector_shard = vector_shard.T
    vector_shards = by_layer(vector_shard)
    weights = []
    for layer in range(2):
        matrices = [gather_rows(pair[layer]) for pair in shards]
        vectors = gather_rows(vector_shards[layer]).T.astype(jnp.float32)
        weights.append((*matrices, vectors[:2], vectors[2:]))

    own_drawn = random_blocks[0]
    sent = lax.dynamic_index_in_dim(own_drawn, 1 - section, 0, keepdims=False)
    kept = pick(own_drawn)
    came = swap(sent, "section", 1)
    tables = (
        listed_blocks(jnp.where(first, kept, came), ctx_index, group_size),
        listed_blocks(jnp.where(first, came, kept), ctx_index, group_size),
    )

    start = pick(tokens)
    output_one, saved_one = layer_forward(start, tables[0], weights[0])
    output_two, saved_two = layer_forward(
        output_one.astype(jnp.bfloat16), tables[1], weights[1]
    )
    chosen = chosen_rows(pick(mask_pos), pick(mask_count), ctx_index, tokens_dev)
    loss_grad = chosen[:, None] * (output_two - pick(targets).astype(jnp.float32))
    grad_two, matrix_grads_two, vector_grads_two = layer_backward(
        loss_grad, saved_two, tables[1], weights[1]
    )
    grad_two_low = lax.optimization_barrier(grad_two.astype(jnp.bfloat16))
    grad_two = grad_two_low.astype(jnp.float32)
    grad_one, matrix_grads_one, vector_grads_one = layer_backward(
        grad_two, saved_one, tables[0], weights[0]
    )

    def own_layer(one, two):
        sent = jnp.where(first, two, one)
        kept = jnp.where(first, one, two)
        return kept + swap(sent.astype(jnp.bfloat16), "section", 1).astype(jnp.float32)

    grads = []
    for one, two in zip(matrix_grads_one, matrix_grads_two):
        two_shard = scatter_rows(two)
        one_shard = scatter_rows(one)
        grads.append(own_layer(one_shard, two_shard))

    sent = jnp.where(first, vector_grads_two, vector_grads_one)
    vectors = jnp.where(first, vector_grads_one, vector_grads_two)
    vectors = vectors + swap(sent, "section", 1)
    for axis in ("ctx", "dp"):
        for bit in bits_of(lax.axis_size(axis)):
            vectors = vectors + swap(vectors, axis, bit)
    width = norm_gain.shape[2]
    place = (lax.axis_index("dp") * group_size + ctx_index) * width
    vectors = lax.dynamic_slice_in_dim(vectors, place, width, axis=1)

    def by_sequence(one, two):
        sent = jnp.where(first, two, one)
        kept = jnp.where(first, one, two)
        came = swap(sent, "section", 1)
        return jnp.stack([jnp.where(first, kept, came), jnp.where(first, came, kept)])[None]

    outputs = by_sequence(output_one, output_two)
    input_grads = by_sequence(grad_one, grad_two)
    return (
        outputs,
        input_grads,
        *[member[None] for member in grads],
        vectors[:2][None],
        vectors[2:][None],
    )


def solution(mesh):
    rows = P("section", ("dp", "ctx"), None)
    columns = P("section", None, ("dp", "ctx"))
    tokens = P("dp", "ctx", None)
    return jax.shard_map(
        body,
        mesh=mesh,
        in_specs=(
            tokens,
            rows,
            rows,
            rows,
            rows,
            columns,
            columns,
            P("section", "dp", None, None, None),
            tokens,
            P("dp", None),
            P("dp"),
        ),
        out_specs=(
            P("section", "dp", "ctx", None),
            P("section", "dp", "ctx", None),
            rows,
            rows,
            rows,
            rows,
            columns,
            columns,
        ),
        check_vma=False,
    )
```
